32 devices in a mesh: dp: 4 (over z), ctx: 8 (over y, x, core).
Axes of the slice: x: 2, y: 2, z: 4, core: 2. Of those that a mesh axis runs over, the one named last changes fastest.
Arguments:
- queries: bfloat16 [8192, 2048], P(('dp', 'ctx')), parts along dimension 0, may hold values from -256 to 256
- key_rows: bfloat16 [8192, 2048], P(('dp', 'ctx')), parts along dimension 0, may hold values from -256 to 256
- values: bfloat16 [8192, 2048], P(('dp', 'ctx')), parts along dimension 0, may hold values from -6 to 6
- inner_rows: bfloat16 [8192, 4096], P(('dp', 'ctx')), parts along dimension 0, may hold values from -6 to 6
- conv_weight: float32 [4, 4096], replicated, may hold values from -3 to 3
- conv_bias: float32 [4096], replicated, may hold values from -3 to 3
- segment_ids: int32 [8192], P(('dp', 'ctx')), parts along dimension 0, may hold values from 0 to 1, never falling along the last dimension, each value on 1 to 2047 neighbouring positions
- block_reach: int32 [64], P(('dp', 'ctx')), parts along dimension 0, may hold values from 128 to 2048
- owner_counts: int32 [32], P('dp'), parts along dimension 0, may hold values from 1 to 3, as said below
Outputs:
- attn_owned: bfloat16 [12288, 2048], P(('dp', 'ctx')), parts along dimension 0
- conv_owned: bfloat16 [12288, 4096], P(('dp', 'ctx')), parts along dimension 0
The draws below stay inside these ranges and needn't reach their ends.
There are 4 independent parts, one for each index of `dp`. The reference program is written for one: setup_inputs(seed, part) draws one part's arguments, and reference() takes and returns one part's arrays. A program takes and returns all parts, laid end to end along the dimension named above; an argument that names none is the same for every part. Nothing has to cross between parts.
Inputs may be any that keep to these rules, and one draw needn't show every extreme that they name: `owner_counts`: the counts sum to 16. The blocks owned by the devices before device d number at least d * 2 and at most d * 2 + 1.
All inputs are finite; a program needn't handle non-finite values.
Results may differ from the reference program's by a relative error of at most 0.0047.
Values may be sent and summed in bfloat16 or wider, within the bound.
A program may use at most 192 MiB of HBM per device.

```python
import math
import jax
import jax.numpy as jnp
import numpy as np
from jax import lax

HEADS = 16
D_HEAD = 128
CH = 4096
WINDOW = 2048
BLOCK = 128
KERNEL = 4
SEQ = 2048
FEAT = 2048
BPD = 2
MAXB = 3
NBLK = 16
DOCS = 2
DOC_MOST = 2047
N_CTX = 8


def attention_pair(key):
    key_draw = jax.random.normal(jax.random.fold_in(key, 101), (SEQ, FEAT), jnp.float32)
    query_draw = jax.random.normal(jax.random.fold_in(key, 102), (SEQ, FEAT), jnp.float32)
    return (query_draw, key_draw)


def draw_queries(key, part):
    return attention_pair(key)[0].astype(jnp.bfloat16)


def draw_key_rows(key, part):
    return attention_pair(key)[1].astype(jnp.bfloat16)


def draw_owner_counts(key, part):
    halfway = BPD // 2
    drift = jax.random.randint(jax.random.fold_in(key, 201), (N_CTX + 1,), 0, halfway + 1)
    widest = jax.random.randint(jax.random.fold_in(key, 202), (), 1, N_CTX - 1)
    places = jnp.arange(N_CTX + 1, dtype=jnp.int32)
    drift = jnp.where(places == widest, 0, drift)
    drift = jnp.where(places == widest + 1, halfway, drift)
    drift = jnp.where(places == widest + 2, 0, drift)
    drift = jnp.where((places == 0) | (places == N_CTX), 0, drift)
    return (BPD + drift[1:] - drift[:-1]).astype(jnp.int32)


def set_ends(values, stream_key, smallest, top_value):
    dims = values.shape
    index_at = [jax.random.randint(jax.random.fold_in(stream_key, axis), (), 0, dims[axis]) for axis in range(len(dims))]
    values = values.at[tuple(index_at)].set(smallest)
    longest = dims.index(max(dims))
    index_at[longest] = (index_at[longest] + 1) % dims[longest]
    return values.at[tuple(index_at)].set(top_value)


def shard_levels(key, dims, cuts, low, high):
    level, own = 1.0, jax.random.fold_in(key, 6)
    for position, blocks in cuts:
        steps = jnp.exp(jax.random.uniform(jax.random.fold_in(own, position), (blocks,), jnp.float32, low / len(cuts), high / len(cuts)))
        level = level * jnp.repeat(steps, dims[position] // blocks).reshape([-1 if axis == position else 1 for axis in range(len(dims))])
    return level


def length_profile(amount, total, reach, skew):
    weights = [(1 << 20) // math.isqrt(grade ** skew) + 1 for grade in range(2, amount + 1)]
    rest, holding = total - reach - (amount - 1), [1] * (amount - 1)
    while rest > 0:
        free = [i for i in range(amount - 1) if holding[i] < reach]
        whole, left = sum([weights[i] for i in free]), rest
        for i in free:
            addition = min(reach - holding[i], max(1, left * weights[i] // whole), rest)
            holding[i] = holding[i] + addition
            rest = rest - addition
    return np.array([reach] + holding)


def ragged(key, amount, total, bound, skew):
    if amount == 2:
        one = jax.random.randint(key, (), max(1, total - bound), min(bound, total - 1) + 1)
        return jnp.stack([one, total - one])
    lengths = jnp.asarray(length_profile(amount, total, bound, skew), jnp.int32)
    twos = (amount - 1) // 2
    donor, taker = lengths[1:1 + 2 * twos:2], lengths[2:2 + 2 * twos:2]
    slack = jnp.minimum(donor - 1, bound - taker)
    moved = jax.random.randint(jax.random.fold_in(key, 1), (twos,), 0, 1 << 20) % (slack + 1)
    lengths = lengths.at[1:1 + 2 * twos:2].set(donor - moved).at[2:2 + 2 * twos:2].set(taker + moved)
    return lengths[jax.random.permutation(jax.random.fold_in(key, 2), amount)]


def scatter_about(key, dims, deviation, reach, split=(), held_as=jnp.bfloat16):
    result = deviation * jax.random.normal(key, dims, jnp.float32)
    if split:
        result = result * shard_levels(key, dims, split, -0.22, 0.18)
    return jnp.clip(result, -reach, reach).astype(held_as)


def setup_inputs(seed: int = 0, part: int = 0) -> dict:
    key_of = jax.random.split(jax.random.key(seed), 10)
    part_keys = jax.random.split(jax.random.fold_in(key_of[9], part), 10)
    queries = draw_queries(jax.random.fold_in(jax.random.fold_in(key_of[9], part), 71), part)
    key_rows = draw_key_rows(jax.random.fold_in(jax.random.fold_in(key_of[9], part), 71), part)
    values = scatter_about(part_keys[2], (SEQ, FEAT), 1.0, 6.0, ((0, 8),))
    inner_rows = scatter_about(part_keys[3], (SEQ, CH), 1.0, 6.0, ((0, 8),))
    conv_weight = scatter_about(key_of[4], (KERNEL, CH), 0.5, 3.0, (), jnp.float32)
    conv_bias = scatter_about(key_of[5], (CH,), 0.5, 3.0, (), jnp.float32)
    segment_ids = jnp.searchsorted(jnp.cumsum(ragged(part_keys[6], DOCS, SEQ, DOC_MOST, 0)), jnp.arange(SEQ), side="right").astype(jnp.int32)
    block_reach = set_ends(jax.random.randint(part_keys[7], (NBLK,), BLOCK, WINDOW + 1), jax.random.fold_in(part_keys[7], 1), BLOCK, WINDOW).astype(jnp.int32)
    owner_counts = draw_owner_counts(jax.random.fold_in(jax.random.fold_in(key_of[9], part), 71), part)
    return dict(queries=queries, key_rows=key_rows, values=values, inner_rows=inner_rows, conv_weight=conv_weight, conv_bias=conv_bias, segment_ids=segment_ids, block_reach=block_reach, owner_counts=owner_counts)


masked_score = -1e+30

def attend(query_rows, key_span, value_span, query_seg, key_seg, block_first, reach_value):
    query_pos = block_first + jnp.arange(BLOCK, dtype=jnp.int32)
    key_pos = block_first - WINDOW + jnp.arange(WINDOW + BLOCK, dtype=jnp.int32)
    allowed = (key_pos[None, :] <= query_pos[:, None]) & (key_pos[None, :] > query_pos[:, None] - WINDOW)
    allowed = allowed & (key_pos[None, :] >= block_first - reach_value) & (key_pos[None, :] >= 0)
    allowed = allowed & (key_seg[None, :] == query_seg[:, None])
    heads_q = query_rows.reshape(BLOCK, HEADS, D_HEAD).astype(jnp.float32)
    heads_k = key_span.reshape(WINDOW + BLOCK, HEADS, D_HEAD).astype(jnp.float32)
    heads_v = value_span.reshape(WINDOW + BLOCK, HEADS, D_HEAD).astype(jnp.float32)
    scores = jnp.einsum('qhd,khd->hqk', heads_q, heads_k) * (1.0 / math.sqrt(D_HEAD))
    scores = jnp.where(allowed[None], scores, masked_score)
    row_top = lax.optimization_barrier(jnp.max(scores, axis=2, keepdims=True))
    lifted = jnp.where(allowed[None], jnp.exp(scores - row_top), 0.0)
    weights = (lifted / lax.optimization_barrier(jnp.sum(lifted, axis=2, keepdims=True))).astype(jnp.bfloat16)
    mixed = jnp.einsum('hqk,khd->qhd', weights.astype(jnp.float32), heads_v)
    return mixed.reshape(BLOCK, HEADS * D_HEAD).astype(jnp.bfloat16)

def convolve(ext_rows, ext_seg, ext_pos, conv_weight, conv_bias, row_count):
    lag = KERNEL - 1
    running = jnp.zeros((row_count, conv_bias.shape[0]), jnp.float32) + conv_bias[None, :]
    for offset in range(KERNEL):
        shifted = ext_rows[lag - offset:lag - offset + row_count].astype(jnp.float32)
        usable = (ext_seg[lag - offset:lag - offset + row_count] == ext_seg[lag:]) & (ext_pos[lag - offset:lag - offset + row_count] >= 0)
        running = running + conv_weight[offset][None, :] * jnp.where(usable[:, None], shifted, 0.0)
    return jax.nn.silu(running).astype(jnp.bfloat16)

def reference(queries, key_rows, values, inner_rows, conv_weight, conv_bias, segment_ids, block_reach, owner_counts):
    seq_len = queries.shape[0]
    features = queries.shape[1]
    lag = KERNEL - 1
    padded_keys = jnp.concatenate([jnp.zeros((WINDOW, features), key_rows.dtype), key_rows], axis=0)
    padded_values = jnp.concatenate([jnp.zeros((WINDOW, features), values.dtype), values], axis=0)
    padded_segs = jnp.concatenate([jnp.full((WINDOW,), -1, jnp.int32), segment_ids.astype(jnp.int32)], axis=0)

    def one_block(block_id):
        block_first = (block_id * BLOCK).astype(jnp.int32)
        query_part = lax.dynamic_slice_in_dim(queries, block_first, BLOCK, 0)
        query_segs = lax.dynamic_slice_in_dim(segment_ids.astype(jnp.int32), block_first, BLOCK, 0)
        key_part = lax.dynamic_slice_in_dim(padded_keys, block_first, WINDOW + BLOCK, 0)
        value_part = lax.dynamic_slice_in_dim(padded_values, block_first, WINDOW + BLOCK, 0)
        key_segs = lax.dynamic_slice_in_dim(padded_segs, block_first, WINDOW + BLOCK, 0)
        return attend(query_part, key_part, value_part, query_segs, key_segs, block_first, block_reach[block_id])
    attention = lax.map(one_block, jnp.arange(NBLK, dtype=jnp.int32)).reshape(seq_len, features)
    ext_rows = jnp.concatenate([jnp.zeros((lag, inner_rows.shape[1]), inner_rows.dtype), inner_rows], axis=0)
    ext_seg = jnp.concatenate([jnp.full((lag,), -1, jnp.int32), segment_ids.astype(jnp.int32)], axis=0)
    ext_pos = jnp.arange(seq_len + lag, dtype=jnp.int32) - lag
    mixed = convolve(ext_rows, ext_seg, ext_pos, conv_weight, conv_bias, seq_len)
    counts = owner_counts.astype(jnp.int32)
    first = (jnp.cumsum(counts) - counts).astype(jnp.int32)
    slot_rows = jnp.arange(MAXB * BLOCK, dtype=jnp.int32)
    token_index = first[:, None] * BLOCK + slot_rows[None, :]
    live = (slot_rows[None, :] < counts[:, None] * BLOCK).reshape(-1)
    token_index = jnp.clip(token_index, 0, seq_len - 1).reshape(-1).astype(jnp.int32)
    attn_owned = jnp.where(live[:, None], attention[token_index], 0).astype(attention.dtype)
    conv_owned = jnp.where(live[:, None], mixed[token_index], 0).astype(mixed.dtype)
    return (attn_owned, conv_owned)
```

```python
import functools
import math

import jax
import jax.numpy as jnp
from jax import lax
from jax.experimental import pallas as pl
from jax.experimental.pallas import tpu as pltpu
from jax.sharding import PartitionSpec as P

HEADS = 16
D_HEAD = 128
WINDOW = 2048
BLOCK = 128
KERNEL = 4


masked_score = -1e30


def from_behind(block, axis, distance):
    devices = range(lax.axis_size(axis))
    route = [(i - distance, i) for i in devices if i - distance in devices]
    return lax.ppermute(block, axis, route)


def attend(query_rows, key_span, value_span, query_seg, key_seg, block_first, reach_value):
    query_pos = block_first + jnp.arange(BLOCK, dtype=jnp.int32)
    key_pos = block_first - WINDOW + jnp.arange(WINDOW + BLOCK, dtype=jnp.int32)
    allowed = (key_pos[None, :] <= query_pos[:, None]) & (
        key_pos[None, :] > query_pos[:, None] - WINDOW
    )
    allowed = allowed & (key_pos[None, :] >= block_first - reach_value) & (key_pos[None, :] >= 0)
    allowed = allowed & (key_seg[None, :] == query_seg[:, None])
    heads_q = query_rows.reshape(BLOCK, HEADS, D_HEAD)
    heads_k = key_span.reshape(WINDOW + BLOCK, HEADS, D_HEAD)
    heads_v = value_span.reshape(WINDOW + BLOCK, HEADS, D_HEAD)
    scores = jnp.einsum("qhd,khd->hqk", heads_q, heads_k, preferred_element_type=jnp.float32) * (
        1.0 / math.sqrt(D_HEAD)
    )
    scores = jnp.where(allowed[None], scores, masked_score)
    row_top = jnp.max(scores, axis=2, keepdims=True)
    lifted = jnp.where(allowed[None], jnp.exp(scores - row_top), 0.0)
    weights = (lifted / jnp.sum(lifted, axis=2, keepdims=True)).astype(jnp.bfloat16)
    mixed = jnp.einsum("hqk,khd->qhd", weights, heads_v, preferred_element_type=jnp.float32)
    return mixed.reshape(BLOCK, HEADS * D_HEAD).astype(jnp.bfloat16)


def convolve(ext_rows, ext_seg, ext_pos, conv_weight, conv_bias, row_count):
    lag = KERNEL - 1
    running = jnp.zeros((row_count, conv_bias.shape[0]), jnp.float32) + conv_bias[None, :]
    for offset in range(KERNEL):
        shifted = ext_rows[lag - offset : lag - offset + row_count].astype(jnp.float32)
        usable = (ext_seg[lag - offset : lag - offset + row_count] == ext_seg[lag:]) & (
            ext_pos[lag - offset : lag - offset + row_count] >= 0
        )
        running = running + conv_weight[offset][None, :] * jnp.where(usable[:, None], shifted, 0.0)
    return jax.nn.silu(running).astype(jnp.bfloat16)


def shards(
    queries,
    key_rows,
    values,
    inner_rows,
    conv_weight,
    conv_bias,
    segment_ids,
    block_reach,
    owner_counts,
):
    here_index = lax.axis_index("ctx")
    row_count = queries.shape[0]
    features = queries.shape[1]
    channels = inner_rows.shape[1]
    per_device = row_count // BLOCK
    most_blocks = per_device + per_device // 2
    back = WINDOW // row_count
    lag = KERNEL - 1
    starts = jnp.cumsum(owner_counts) - owner_counts
    first_block = starts[here_index]
    own_blocks = owner_counts[here_index]
    live = jnp.arange(most_blocks * BLOCK, dtype=jnp.int32) < own_blocks * BLOCK
    far_keys = []
    far_values = []
    far_segments = []
    for distance in range(back, 0, -1):
        received = from_behind((key_rows, values, segment_ids), "ctx", distance)
        far_keys.append(received[0])
        far_values.append(received[1])
        far_segments.append(received[2])
    key_buffer = jnp.concatenate(far_keys + [key_rows], axis=0)
    value_buffer = jnp.concatenate(far_values + [values], axis=0)
    segment_buffer = jnp.concatenate(far_segments + [segment_ids], axis=0)
    key_anchor = (here_index - back) * row_count
    tail_rows, tail_segments = from_behind(
        (inner_rows[row_count - lag :], segment_ids[row_count - lag :]), "ctx", 1
    )

    def own_block(slot_index):
        local_first = slot_index * BLOCK
        block_first = here_index * row_count + local_first
        key_at = block_first - WINDOW - key_anchor
        return attend(
            lax.dynamic_slice_in_dim(queries, local_first, BLOCK, 0),
            lax.dynamic_slice_in_dim(key_buffer, key_at, WINDOW + BLOCK, 0),
            lax.dynamic_slice_in_dim(value_buffer, key_at, WINDOW + BLOCK, 0),
            lax.dynamic_slice_in_dim(segment_ids, local_first, BLOCK, 0),
            lax.dynamic_slice_in_dim(segment_buffer, key_at, WINDOW + BLOCK, 0),
            block_first,
            block_reach[slot_index],
        )

    attention_local = lax.map(own_block, jnp.arange(per_device, dtype=jnp.int32)).reshape(
        row_count, features
    )
    conv_local = convolve(
        jnp.concatenate([tail_rows, inner_rows], axis=0),
        jnp.concatenate([tail_segments, segment_ids], axis=0),
        here_index * row_count - lag + jnp.arange(row_count + lag, dtype=jnp.int32),
        conv_weight,
        conv_bias,
        row_count,
    )
    above = from_behind((attention_local, conv_local), "ctx", -1)
    attention_near = jnp.concatenate(
        [attention_local, above[0], jnp.zeros((row_count, features), jnp.bfloat16)], axis=0
    )
    conv_near = jnp.concatenate(
        [conv_local, above[1], jnp.zeros((row_count, channels), jnp.bfloat16)], axis=0
    )
    offset_rows = first_block * BLOCK - here_index * row_count
    attention_owned = lax.dynamic_slice_in_dim(attention_near, offset_rows, most_blocks * BLOCK, 0)
    conv_owned_rows = lax.dynamic_slice_in_dim(conv_near, offset_rows, most_blocks * BLOCK, 0)
    attention_owned = jnp.where(live[:, None], attention_owned, 0)
    conv_owned_rows = jnp.where(live[:, None], conv_owned_rows, 0)
    return (attention_owned, conv_owned_rows)


LANES = 128
HALO = 16
MESH = pl.DeviceIdType.MESH


def partner(me, offset, n):
    result, bit = 0, 1
    while bit < n:
        result = result + ((me // bit + offset // bit) % 2) * bit
        bit *= 2
    return result


def exchange_kernel(
    n,
    row_count,
    head_count,
    q_hbm,
    k_hbm,
    v_hbm,
    x_hbm,
    weight_ref,
    bias_ref,
    info_ref,
    attn_near,
    conv_near,
    qr,
    kr,
    vr,
    ob,
    xb,
    infos,
    start_ref,
    lo_ref,
    s_ref,
    qkv_send,
    qkv_recv,
    o_send,
    o_recv,
    info_send,
    info_recv,
    halo_sem,
    local_sem,
):
    me = lax.axis_index("ctx")
    per_device = row_count // BLOCK
    near = row_count + BLOCK
    seq_len = n * row_count
    channels = bias_ref.shape[1]
    chunk = s_ref.shape[2]
    scale = math.log2(math.e) / math.sqrt(D_HEAD)
    order = list(range(2, n)) + [1]

    barrier = pltpu.get_barrier_semaphore()
    for offset in range(1, n):
        pl.semaphore_signal(
            barrier, inc=1, device_id={"ctx": partner(me, offset, n)}, device_id_type=MESH
        )
    pl.semaphore_wait(barrier, n - 1)

    def rows_of(device, count=row_count):
        return pl.ds(pl.multiple_of(device * row_count, BLOCK), count)

    def head_of(device, head):
        at = device * (head_count * D_HEAD) + head * D_HEAD
        return pl.ds(pl.multiple_of(at, D_HEAD), D_HEAD)

    def remote(src, dst, send, recv, device):
        return pltpu.make_async_remote_copy(
            src_ref=src,
            dst_ref=dst,
            send_sem=send,
            recv_sem=recv,
            device_id={"ctx": device},
            device_id_type=MESH,
        )

    def info_copy(offset):
        return remote(
            info_ref,
            infos.at[me],
            info_send.at[offset],
            info_recv.at[offset],
            partner(me, offset, n),
        )

    pairs = ((k_hbm, kr), (q_hbm, qr), (v_hbm, vr))

    def qkv_copy(which, head, offset):
        peer = partner(me, offset, n)
        src, dst = pairs[which]
        return remote(
            src.at[:, head_of(peer, head)],
            dst.at[head, rows_of(me)],
            qkv_send.at[which, head, offset],
            qkv_recv.at[which, head, offset],
            peer,
        )

    def own_copy(which, head):
        src, dst = pairs[which]
        return pltpu.make_async_copy(
            src.at[:, head_of(me, head)], dst.at[head, rows_of(me)], local_sem.at[which, head]
        )

    tail_copy = remote(
        x_hbm.at[pl.ds(row_count - HALO, HALO)],
        xb.at[pl.ds(0, HALO)],
        halo_sem.at[0],
        halo_sem.at[1],
        (me + 1) % n,
    )
    above_copy = remote(
        x_hbm.at[pl.ds(0, BLOCK)],
        xb.at[pl.ds(HALO + row_count, BLOCK)],
        halo_sem.at[2],
        halo_sem.at[3],
        (me + n - 1) % n,
    )
    own_rows = pltpu.make_async_copy(x_hbm, xb.at[pl.ds(HALO, row_count)], halo_sem.at[4])

    for offset in order:
        info_copy(offset).start()

    @pl.when(me < n - 1)
    def _():
        tail_copy.start()

    own_rows.start()
    for head in range(head_count):
        for which in range(3):
            for offset in order:
                qkv_copy(which, head, offset).start()
            own_copy(which, head).start()

    @pl.when(me > 0)
    def _():
        above_copy.start()

    infos[me] = info_ref[...]
    ob[:, pl.ds(seq_len, BLOCK), :] = jnp.zeros((head_count, BLOCK, D_HEAD), ob.dtype)
    start_ref[pl.ds(seq_len, BLOCK), :] = jnp.zeros((BLOCK, LANES), jnp.int32)

    @pl.when(me == 0)
    def _():
        xb[pl.ds(0, HALO), :] = jnp.zeros((HALO, channels), xb.dtype)

    @pl.when(me == n - 1)
    def _():
        xb[pl.ds(HALO + row_count, BLOCK), :] = jnp.zeros((BLOCK, channels), xb.dtype)

    for offset in order:
        info_copy(offset).wait()

    def bounds(device, carry):
        for part in range(per_device):
            segs = jnp.broadcast_to(infos[device, part : part + 1, :], (BLOCK, LANES)).T
            reach = infos[device, per_device + part : per_device + part + 1, :]
            count = jnp.zeros((BLOCK, LANES), jnp.float32)
            for other in range(n):
                for row in range(per_device):
                    count = count + jnp.where(infos[other, row : row + 1, :] < segs, 1.0, 0.0)
            begin = jnp.broadcast_to(
                jnp.sum(count, axis=1, keepdims=True), (BLOCK, LANES)
            ).astype(jnp.int32)
            first = device * row_count + part * BLOCK
            at = pl.ds(pl.multiple_of(first, BLOCK), BLOCK)
            start_ref[at, :] = begin
            lo_ref[at, :] = jnp.maximum(begin, first - reach)
        return carry

    lax.fori_loop(0, n, bounds, 0)

    def convolve_block(block):
        first = me * row_count + block * BLOCK
        begin = start_ref[pl.ds(pl.multiple_of(first, BLOCK), BLOCK), :]
        place = first + lax.broadcasted_iota(jnp.int32, (BLOCK, LANES), 0) - begin

        def part(step, carry):
            cols = pl.ds(pl.multiple_of(step * LANES, LANES), LANES)
            rows = xb[pl.ds(block * BLOCK, BLOCK + HALO), cols].astype(jnp.float32)
            running = jnp.broadcast_to(bias_ref[:, cols], (BLOCK, LANES))
            for tap in range(KERNEL):
                moved = rows if tap == 0 else pltpu.roll(rows, tap, 0)
                moved = moved[HALO:]
                if tap:
                    moved = jnp.where(place >= tap, moved, 0.0)
                running = running + weight_ref[tap : tap + 1, cols] * moved
            gated = running / (1.0 + jnp.exp(-running))
            conv_near[pl.ds(block * BLOCK, BLOCK), cols] = gated.astype(conv_near.dtype)
            return carry

        lax.fori_loop(0, channels // LANES, part, 0)

    own_rows.wait()

    @pl.when(me > 0)
    def _():
        tail_copy.wait_recv()

    for block in range(per_device):
        convolve_block(block)

    def attend_rows(head, owner):
        q = qr[head, rows_of(owner), :]
        lo = lo_ref[rows_of(owner), :]
        place = owner * row_count + lax.broadcasted_iota(jnp.int32, (row_count, LANES), 0)
        lane = lax.broadcasted_iota(jnp.int32, (row_count, LANES), 1)
        steps = (owner * row_count + row_count + chunk - 1) // chunk

        def score(step, top):
            keys = kr[head, pl.ds(pl.multiple_of(step * chunk, chunk), chunk), :]
            scores = lax.dot_general(
                q, keys, (((1,), (1,)), ((), ())), preferred_element_type=jnp.float32
            )
            for group in range(chunk // LANES):
                at = step * chunk + group * LANES + lane
                masked = jnp.where(
                    (at >= lo) & (at <= place),
                    scores[:, group * LANES : (group + 1) * LANES],
                    masked_score,
                )
                s_ref[step, :, pl.ds(group * LANES, LANES)] = masked
                top = jnp.maximum(top, masked)
            return top

        top = lax.fori_loop(
            0, steps, score, jnp.full((row_count, LANES), masked_score, jnp.float32)
        )
        top = jnp.broadcast_to(jnp.max(top, axis=1, keepdims=True), (row_count, LANES))

        def blend(step, carry):
            total, mixed = carry
            weights = []
            for group in range(chunk // LANES):
                scores = s_ref[step, :, pl.ds(group * LANES, LANES)]
                lifted = jnp.exp2((scores - top) * scale)
                total = total + lifted
                weights.append(lifted.astype(jnp.bfloat16))
            vals = vr[head, pl.ds(pl.multiple_of(step * chunk, chunk), chunk), :]
            mixed = mixed + jnp.dot(
                jnp.concatenate(weights, axis=1), vals, preferred_element_type=jnp.float32
            )
            return total, mixed

        zero = jnp.zeros((row_count, LANES), jnp.float32)
        total, mixed = lax.fori_loop(0, steps, blend, (zero, zero))
        mixed = mixed / jnp.sum(total, axis=1, keepdims=True)
        ob[head, rows_of(owner), :] = mixed.astype(ob.dtype)

    def out_copy(head, offset):
        peer = partner(me, offset, n)
        return remote(
            ob.at[head, rows_of(peer, near)],
            attn_near.at[:, head_of(me, head)],
            o_send.at[head, offset],
            o_recv.at[head, offset],
            peer,
        )

    def own_out(head):
        return pltpu.make_async_copy(
            ob.at[head, rows_of(me, near)], attn_near.at[:, head_of(me, head)], local_sem.at[3, head]
        )

    for head in range(head_count):
        for which in range(3):
            own_copy(which, head).wait()
            for offset in order:
                qkv_copy(which, head, offset).wait_recv()

        def each(step, carry):
            attend_rows(head, partner(me, (step + 2) % n, n))
            return carry

        lax.fori_loop(0, n, each, 0)
        for offset in order:
            out_copy(head, offset).start()
        own_out(head).start()

    @pl.when(me < n - 1)
    def _():
        above_copy.wait_recv()

    convolve_block(per_device)

    for head in range(head_count):
        own_out(head).wait()
        for offset in order:
            out_copy(head, offset).wait()
            for which in range(3):
                qkv_copy(which, head, offset).wait_send()

    @pl.when(me < n - 1)
    def _():
        tail_copy.wait_send()

    @pl.when(me > 0)
    def _():
        above_copy.wait_send()


def exchange(n, queries, key_rows, values, inner_rows, conv_weight, conv_bias, info):
    row_count, features = queries.shape
    channels = inner_rows.shape[1]
    head_count = features // (n * D_HEAD)
    seq_len = n * row_count
    near = row_count + BLOCK
    chunk = 2 * row_count if n % 2 == 0 else row_count
    dtype = queries.dtype
    hbm = pl.BlockSpec(memory_space=pl.ANY)
    vmem = pl.BlockSpec(memory_space=pltpu.VMEM)
    return pl.pallas_call(
        functools.partial(exchange_kernel, n, row_count, head_count),
        out_shape=(
            jax.ShapeDtypeStruct((near, features), dtype),
            jax.ShapeDtypeStruct((near, channels), dtype),
        ),
        in_specs=[hbm, hbm, hbm, hbm, vmem, vmem, vmem],
        out_specs=(hbm, vmem),
        scratch_shapes=[
            pltpu.VMEM((head_count, seq_len, D_HEAD), dtype),
            pltpu.VMEM((head_count, seq_len, D_HEAD), dtype),
            pltpu.VMEM((head_count, seq_len, D_HEAD), dtype),
            pltpu.VMEM((head_count, seq_len + BLOCK, D_HEAD), dtype),
            pltpu.VMEM((HALO + near, channels), dtype),
            pltpu.VMEM((n,) + info.shape, jnp.int32),
            pltpu.VMEM((seq_len + BLOCK, LANES), jnp.int32),
            pltpu.VMEM((seq_len, LANES), jnp.int32),
            pltpu.VMEM((seq_len // chunk, row_count, chunk), jnp.float32),
            pltpu.SemaphoreType.DMA((3, head_count, n)),
            pltpu.SemaphoreType.DMA((3, head_count, n)),
            pltpu.SemaphoreType.DMA((head_count, n)),
            pltpu.SemaphoreType.DMA((head_count, n)),
            pltpu.SemaphoreType.DMA((n,)),
            pltpu.SemaphoreType.DMA((n,)),
            pltpu.SemaphoreType.DMA((5,)),
            pltpu.SemaphoreType.DMA((4, head_count)),
        ],
        compiler_params=pltpu.CompilerParams(
            collective_id=0, has_side_effects=True, vmem_limit_bytes=56 * 1024 * 1024
        ),
    )(queries, key_rows, values, inner_rows, conv_weight, conv_bias, info)


def by_heads(
    queries,
    key_rows,
    values,
    inner_rows,
    conv_weight,
    conv_bias,
    segment_ids,
    block_reach,
    owner_counts,
):
    n = lax.axis_size("ctx")
    here = lax.axis_index("ctx")
    row_count = queries.shape[0]
    per_device = row_count // BLOCK
    near = row_count + BLOCK
    info = jnp.concatenate(
        [
            segment_ids.reshape(per_device, BLOCK),
            jnp.broadcast_to(block_reach[:, None], (per_device, BLOCK)),
            jnp.zeros((-2 * per_device % 8, BLOCK), jnp.int32),
        ],
        axis=0,
    )
    attn_near, conv_near = exchange(
        n, queries, key_rows, values, inner_rows, conv_weight, conv_bias[None, :], info
    )
    device = jnp.arange(n, dtype=jnp.int32)
    first = jnp.sum(jnp.where(device < here, owner_counts, 0))
    own = jnp.sum(jnp.where(device == here, owner_counts, 0))
    moved = first > here * per_device
    live = jnp.arange(near, dtype=jnp.int32) < own * BLOCK

    def owned(rows):
        shifted = jnp.pad(rows[BLOCK:], ((0, BLOCK), (0, 0)))
        return jnp.where(live[:, None], jnp.where(moved, shifted, rows), 0)

    return owned(attn_near), owned(conv_near)


def plan(*args):
    n = lax.axis_size("ctx")
    row_count, features = args[0].shape
    heads = features // D_HEAD
    power = n > 2 and n & (n - 1) == 0
    near_layout = row_count // BLOCK + (row_count // BLOCK) // 2 == row_count // BLOCK + 1
    if power and near_layout and heads % n == 0 and n * row_count <= WINDOW:
        return by_heads(*args)
    return shards(*args)


def solution(mesh):
    return jax.shard_map(
        plan,
        mesh=mesh,
        in_specs=(
            P(("dp", "ctx"), None),
            P(("dp", "ctx"), None),
            P(("dp", "ctx"), None),
            P(("dp", "ctx"), None),
            P(),
            P(),
            P(("dp", "ctx")),
            P(("dp", "ctx")),
            P("dp"),
        ),
        out_specs=(P(("dp", "ctx"), None), P(("dp", "ctx"), None)),
        check_vma=False,
    )
```

```python
import functools
import math

import jax
import jax.numpy as jnp
from jax import lax
from jax.experimental import pallas as pl
from jax.experimental.pallas import tpu as pltpu
from jax.sharding import PartitionSpec as P

HEADS = 16
D_HEAD = 128
WINDOW = 2048
BLOCK = 128
KERNEL = 4


masked_score = -1e30


def from_behind(block, axis, distance):
    devices = range(lax.axis_size(axis))
    route = [(i - distance, i) for i in devices if i - distance in devices]
    return lax.ppermute(block, axis, route)


def attend(query_rows, key_span, value_span, query_seg, key_seg, block_first, reach_value):
    query_pos = block_first + jnp.arange(BLOCK, dtype=jnp.int32)
    key_pos = block_first - WINDOW + jnp.arange(WINDOW + BLOCK, dtype=jnp.int32)
    allowed = (key_pos[None, :] <= query_pos[:, None]) & (
        key_pos[None, :] > query_pos[:, None] - WINDOW
    )
    allowed = allowed & (key_pos[None, :] >= block_first - reach_value) & (key_pos[None, :] >= 0)
    allowed = allowed & (key_seg[None, :] == query_seg[:, None])
    heads_q = query_rows.reshape(BLOCK, HEADS, D_HEAD)
    heads_k = key_span.reshape(WINDOW + BLOCK, HEADS, D_HEAD)
    heads_v = value_span.reshape(WINDOW + BLOCK, HEADS, D_HEAD)
    scores = jnp.einsum("qhd,khd->hqk", heads_q, heads_k, preferred_element_type=jnp.float32) * (
        1.0 / math.sqrt(D_HEAD)
    )
    scores = jnp.where(allowed[None], scores, masked_score)
    row_top = jnp.max(scores, axis=2, keepdims=True)
    lifted = jnp.where(allowed[None], jnp.exp(scores - row_top), 0.0)
    weights = (lifted / jnp.sum(lifted, axis=2, keepdims=True)).astype(jnp.bfloat16)
    mixed = jnp.einsum("hqk,khd->qhd", weights, heads_v, preferred_element_type=jnp.float32)
    return mixed.reshape(BLOCK, HEADS * D_HEAD).astype(jnp.bfloat16)


def convolve(ext_rows, ext_seg, ext_pos, conv_weight, conv_bias, row_count):
    lag = KERNEL - 1
    running = jnp.zeros((row_count, conv_bias.shape[0]), jnp.float32) + conv_bias[None, :]
    for offset in range(KERNEL):
        shifted = ext_rows[lag - offset : lag - offset + row_count].astype(jnp.float32)
        usable = (ext_seg[lag - offset : lag - offset + row_count] == ext_seg[lag:]) & (
            ext_pos[lag - offset : lag - offset + row_count] >= 0
        )
        running = running + conv_weight[offset][None, :] * jnp.where(usable[:, None], shifted, 0.0)
    return jax.nn.silu(running).astype(jnp.bfloat16)


def shards(
    queries,
    key_rows,
    values,
    inner_rows,
    conv_weight,
    conv_bias,
    segment_ids,
    block_reach,
    owner_counts,
):
    here_index = lax.axis_index("ctx")
    row_count = queries.shape[0]
    features = queries.shape[1]
    channels = inner_rows.shape[1]
    per_device = row_count // BLOCK
    most_blocks = per_device + per_device // 2
    back = WINDOW // row_count
    lag = KERNEL - 1
    starts = jnp.cumsum(owner_counts) - owner_counts
    first_block = starts[here_index]
    own_blocks = owner_counts[here_index]
    live = jnp.arange(most_blocks * BLOCK, dtype=jnp.int32) < own_blocks * BLOCK
    far_keys = []
    far_values = []
    far_segments = []
    for distance in range(back, 0, -1):
        received = from_behind((key_rows, values, segment_ids), "ctx", distance)
        far_keys.append(received[0])
        far_values.append(received[1])
        far_segments.append(received[2])
    key_buffer = jnp.concatenate(far_keys + [key_rows], axis=0)
    value_buffer = jnp.concatenate(far_values + [values], axis=0)
    segment_buffer = jnp.concatenate(far_segments + [segment_ids], axis=0)
    key_anchor = (here_index - back) * row_count
    tail_rows, tail_segments = from_behind(
        (inner_rows[row_count - lag :], segment_ids[row_count - lag :]), "ctx", 1
    )

    def own_block(slot_index):
        local_first = slot_index * BLOCK
        block_first = here_index * row_count + local_first
        key_at = block_first - WINDOW - key_anchor
        return attend(
            lax.dynamic_slice_in_dim(queries, local_first, BLOCK, 0),
            lax.dynamic_slice_in_dim(key_buffer, key_at, WINDOW + BLOCK, 0),
            lax.dynamic_slice_in_dim(value_buffer, key_at, WINDOW + BLOCK, 0),
            lax.dynamic_slice_in_dim(segment_ids, local_first, BLOCK, 0),
            lax.dynamic_slice_in_dim(segment_buffer, key_at, WINDOW + BLOCK, 0),
            block_first,
            block_reach[slot_index],
        )

    attention_local = lax.map(own_block, jnp.arange(per_device, dtype=jnp.int32)).reshape(
        row_count, features
    )
    conv_local = convolve(
        jnp.concatenate([tail_rows, inner_rows], axis=0),
        jnp.concatenate([tail_segments, segment_ids], axis=0),
        here_index * row_count - lag + jnp.arange(row_count + lag, dtype=jnp.int32),
        conv_weight,
        conv_bias,
        row_count,
    )
    above = from_behind((attention_local, conv_local), "ctx", -1)
    attention_near = jnp.concatenate(
        [attention_local, above[0], jnp.zeros((row_count, features), jnp.bfloat16)], axis=0
    )
    conv_near = jnp.concatenate(
        [conv_local, above[1], jnp.zeros((row_count, channels), jnp.bfloat16)], axis=0
    )
    offset_rows = first_block * BLOCK - here_index * row_count
    attention_owned = lax.dynamic_slice_in_dim(attention_near, offset_rows, most_blocks * BLOCK, 0)
    conv_owned_rows = lax.dynamic_slice_in_dim(conv_near, offset_rows, most_blocks * BLOCK, 0)
    attention_owned = jnp.where(live[:, None], attention_owned, 0)
    conv_owned_rows = jnp.where(live[:, None], conv_owned_rows, 0)
    return (attention_owned, conv_owned_rows)


LANES = 128
HALO = 16
PAIR = 2
MESH = pl.DeviceIdType.MESH


def partner(me, offset, n):
    result, bit = 0, 1
    while bit < n:
        result = result + ((me // bit + offset // bit) % 2) * bit
        bit *= 2
    return result


def exchange_kernel(
    n,
    row_count,
    head_count,
    q_hbm,
    k_hbm,
    v_hbm,
    x_hbm,
    weight_ref,
    bias_ref,
    info_ref,
    attn_near,
    conv_near,
    qr,
    kr,
    vr,
    ob,
    xb,
    conv_buf,
    q_full,
    k_full,
    v_full,
    o_full,
    infos,
    start_ref,
    lo_ref,
    s_ref,
    qkv_send,
    qkv_recv,
    o_send,
    o_recv,
    extra_send,
    extra_recv,
    pass_send,
    pass_recv,
    full_sem,
    info_send,
    info_recv,
    halo_sem,
    local_sem,
):
    me = lax.axis_index("ctx")
    per_device = row_count // BLOCK
    seq_len = n * row_count
    channels = bias_ref.shape[1]
    chunk = s_ref.shape[2]
    scale = math.log2(math.e) / math.sqrt(D_HEAD)
    order = list(range(2, n)) + [1]

    barrier = pltpu.get_barrier_semaphore()
    for offset in range(1, n):
        pl.semaphore_signal(
            barrier, inc=1, device_id={"ctx": partner(me, offset, n)}, device_id_type=MESH
        )
    pl.semaphore_wait(barrier, n - 1)

    def rows_of(device, count=row_count):
        return pl.ds(pl.multiple_of(device * row_count, BLOCK), count)

    def head_of(device, head):
        at = device * (head_count * D_HEAD) + head * D_HEAD
        return pl.ds(pl.multiple_of(at, D_HEAD), D_HEAD)

    def remote(src, dst, send, recv, device):
        return pltpu.make_async_remote_copy(
            src_ref=src,
            dst_ref=dst,
            send_sem=send,
            recv_sem=recv,
            device_id={"ctx": device},
            device_id_type=MESH,
        )

    def info_copy(offset):
        return remote(
            info_ref,
            infos.at[me],
            info_send.at[offset],
            info_recv.at[offset],
            partner(me, offset, n),
        )

    pairs = ((k_hbm, kr), (q_hbm, qr), (v_hbm, vr))

    def qkv_copy(which, head, offset):
        peer = partner(me, offset, n)
        src, dst = pairs[which]
        return remote(
            src.at[:, head_of(peer, head)],
            dst.at[head, rows_of(me)],
            qkv_send.at[which, head, offset],
            qkv_recv.at[which, head, offset],
            peer,
        )

    def own_copy(which, head):
        src, dst = pairs[which]
        return pltpu.make_async_copy(
            src.at[:, head_of(me, head)], dst.at[head, rows_of(me)], local_sem.at[which, head]
        )

    tail_copy = remote(
        x_hbm.at[pl.ds(row_count - HALO, HALO)],
        xb.at[pl.ds(0, HALO)],
        halo_sem.at[0],
        halo_sem.at[1],
        (me + 1) % n,
    )
    above_copy = remote(
        x_hbm.at[pl.ds(0, BLOCK)],
        xb.at[pl.ds(HALO + row_count, BLOCK)],
        halo_sem.at[2],
        halo_sem.at[3],
        (me + n - 1) % n,
    )
    full_copies = [
        pltpu.make_async_copy(q_hbm, q_full, full_sem.at[0]),
        pltpu.make_async_copy(k_hbm, k_full.at[rows_of(me % PAIR)], full_sem.at[1]),
        pltpu.make_async_copy(v_hbm, v_full.at[rows_of(me % PAIR)], full_sem.at[2]),
    ]
    pair_copies = [
        remote(
            src,
            dst.at[pl.ds(0, row_count)],
            full_sem.at[3 + 2 * i],
            full_sem.at[4 + 2 * i],
            partner(me, 1, n),
        )
        for i, (src, dst) in enumerate(((k_hbm, k_full), (v_hbm, v_full)))
    ]

    def sends(which, device):
        return device >= (PAIR if which == 1 else 0)

    own_rows = pltpu.make_async_copy(x_hbm, xb.at[pl.ds(HALO, row_count)], halo_sem.at[4])

    for offset in order:
        info_copy(offset).start()

    @pl.when(me < n - 1)
    def _():
        tail_copy.start()

    own_rows.start()
    @pl.when(me < PAIR)
    def _():
        for copy in full_copies:
            copy.start()

    @pl.when(me == 0)
    def _():
        for copy in pair_copies:
            copy.start()

    for head in range(head_count):
        for which in range(3):
            for offset in order:

                @pl.when(sends(which, me))
                def _():
                    qkv_copy(which, head, offset).start()

            own_copy(which, head).start()

    @pl.when(me > 0)
    def _():
        above_copy.start()

    infos[me] = info_ref[...]
    start_ref[pl.ds(seq_len, BLOCK), :] = jnp.zeros((BLOCK, LANES), jnp.int32)

    @pl.when(me == 0)
    def _():
        xb[pl.ds(0, HALO), :] = jnp.zeros((HALO, channels), xb.dtype)
        v_full[pl.ds(row_count, row_count), :] = jnp.zeros(q_full.shape, v_full.dtype)

    @pl.when(me == n - 1)
    def _():
        xb[pl.ds(HALO + row_count, BLOCK), :] = jnp.zeros((BLOCK, channels), xb.dtype)

    for offset in order:
        info_copy(offset).wait()

    def bounds(device, carry):
        for part in range(per_device):
            segs = jnp.broadcast_to(infos[device, part : part + 1, :], (BLOCK, LANES)).T
            reach = infos[device, per_device + part : per_device + part + 1, :]
            count = jnp.zeros((BLOCK, LANES), jnp.float32)
            for other in range(n):
                for row in range(per_device):
                    count = count + jnp.where(infos[other, row : row + 1, :] < segs, 1.0, 0.0)
            begin = jnp.broadcast_to(
                jnp.sum(count, axis=1, keepdims=True), (BLOCK, LANES)
            ).astype(jnp.int32)
            first = device * row_count + part * BLOCK
            at = pl.ds(pl.multiple_of(first, BLOCK), BLOCK)
            start_ref[at, :] = begin
            lo_ref[at, :] = jnp.maximum(begin, first - reach)
        return carry

    lax.fori_loop(0, n, bounds, 0)

    def convolve_block(block):
        first = me * row_count + block * BLOCK
        begin = start_ref[pl.ds(pl.multiple_of(first, BLOCK), BLOCK), :]
        place = first + lax.broadcasted_iota(jnp.int32, (BLOCK, LANES), 0) - begin

        def part(step, carry):
            cols = pl.ds(pl.multiple_of(step * LANES, LANES), LANES)
            rows = xb[pl.ds(block * BLOCK, BLOCK + HALO), cols].astype(jnp.float32)
            running = jnp.broadcast_to(bias_ref[:, cols], (BLOCK, LANES))
            for tap in range(KERNEL):
                moved = rows if tap == 0 else pltpu.roll(rows, tap, 0)
                moved = moved[HALO:]
                if tap:
                    moved = jnp.where(place >= tap, moved, 0.0)
                running = running + weight_ref[tap : tap + 1, cols] * moved
            gated = running / (1.0 + jnp.exp(-running))
            conv_buf[pl.ds(block * BLOCK, BLOCK), cols] = gated.astype(conv_buf.dtype)
            return carry

        lax.fori_loop(0, channels // LANES, part, 0)

    own_rows.wait()

    @pl.when(me > 0)
    def _():
        tail_copy.wait_recv()

    for block in range(per_device):
        convolve_block(block)

    def conv_out(at, count, sem):
        rows = pl.ds(at, count)
        return pltpu.make_async_copy(conv_buf.at[rows], conv_near.at[rows], halo_sem.at[sem])

    conv_out(0, row_count, 5).start()

    def attend_rows(q, keys_at, values_at, owner):
        lo = lo_ref[rows_of(owner), :]
        place = owner * row_count + lax.broadcasted_iota(jnp.int32, (row_count, LANES), 0)
        lane = lax.broadcasted_iota(jnp.int32, (row_count, LANES), 1)
        steps = (owner * row_count + row_count + chunk - 1) // chunk

        def score(step, top):
            keys = keys_at(pl.ds(pl.multiple_of(step * chunk, chunk), chunk))
            scores = lax.dot_general(
                q, keys, (((1,), (1,)), ((), ())), preferred_element_type=jnp.float32
            )
            for group in range(chunk // LANES):
                at = step * chunk + group * LANES + lane
                masked = jnp.where(
                    (at >= lo) & (at <= place),
                    scores[:, group * LANES : (group + 1) * LANES],
                    masked_score,
                )
                s_ref[step, :, pl.ds(group * LANES, LANES)] = masked
                top = jnp.maximum(top, masked)
            return top

        top = lax.fori_loop(
            0, steps, score, jnp.full((row_count, LANES), masked_score, jnp.float32)
        )
        top = jnp.broadcast_to(jnp.max(top, axis=1, keepdims=True), (row_count, LANES))

        def blend(step, carry):
            total, mixed = carry
            weights = []
            for group in range(chunk // LANES):
                scores = s_ref[step, :, pl.ds(group * LANES, LANES)]
                lifted = jnp.exp2((scores - top) * scale)
                total = total + lifted
                weights.append(lifted.astype(jnp.bfloat16))
            vals = values_at(pl.ds(pl.multiple_of(step * chunk, chunk), chunk))
            mixed = mixed + jnp.dot(
                jnp.concatenate(weights, axis=1), vals, preferred_element_type=jnp.float32
            )
            return total, mixed

        zero = jnp.zeros((row_count, LANES), jnp.float32)
        total, mixed = lax.fori_loop(0, steps, blend, (zero, zero))
        mixed = mixed / jnp.sum(total, axis=1, keepdims=True)
        return mixed.astype(jnp.bfloat16)

    own_rows_at = pl.ds(0, row_count)
    extra_at = pl.ds(row_count, BLOCK)
    full_out = pltpu.make_async_copy(o_full, attn_near.at[own_rows_at], full_sem.at[7])

    @pl.when(me < PAIR)
    def _():
        for copy in full_copies:
            copy.wait()

        @pl.when(me == 1)
        def _():
            for copy in pair_copies:
                copy.wait_recv()

        def each(head, carry):
            cols = pl.ds(pl.multiple_of(head * D_HEAD, D_HEAD), D_HEAD)
            o_full[:, cols] = attend_rows(
                q_full[:, cols], lambda at: k_full[at, cols], lambda at: v_full[at, cols], me
            )
            return carry

        lax.fori_loop(0, n * head_count, each, 0)
        full_out.start()

    def out_copy(head, offset):
        peer = partner(me, offset, n)
        return remote(
            ob.at[head, rows_of(peer)],
            attn_near.at[own_rows_at, head_of(me, head)],
            o_send.at[head, offset],
            o_recv.at[head, offset],
            peer,
        )

    def extra_copy(head, offset):
        peer = partner(me, offset, n)
        return remote(
            ob.at[head, rows_of((peer + 1) % n, BLOCK)],
            attn_near.at[extra_at, head_of(me, head)],
            extra_send.at[head, offset],
            extra_recv.at[head, offset],
            peer,
        )

    def own_out(head):
        return pltpu.make_async_copy(
            ob.at[head, rows_of(me)],
            attn_near.at[own_rows_at, head_of(me, head)],
            local_sem.at[3, head],
        )

    def own_extra(head):
        return pltpu.make_async_copy(
            ob.at[head, rows_of((me + 1) % n, BLOCK)],
            attn_near.at[extra_at, head_of(me, head)],
            local_sem.at[4, head],
        )

    def pass_copy(offset):
        at = partner(me, offset, n) * (head_count * D_HEAD)
        cols = pl.ds(pl.multiple_of(at, D_HEAD), head_count * D_HEAD)
        return remote(
            attn_near.at[pl.ds(0, BLOCK), cols],
            attn_near.at[extra_at, cols],
            pass_send.at[offset],
            pass_recv.at[offset],
            partner(me, 1, n),
        )

    def far(device):
        return device >= PAIR

    def extra(device):
        return (device % PAIR == PAIR - 1) & (device < n - 1)

    odd = me % PAIR == PAIR - 1

    for head in range(head_count):
        for which in range(3):
            own_copy(which, head).wait()
            for offset in order:

                @pl.when(sends(which, partner(me, offset, n)))
                def _():
                    qkv_copy(which, head, offset).wait_recv()

        def each(step, carry):
            owner = partner(me, (step + 2) % n, n)

            @pl.when(far(owner))
            def _():
                ob[head, rows_of(owner), :] = attend_rows(
                    qr[head, rows_of(owner), :],
                    lambda at: kr[head, at, :],
                    lambda at: vr[head, at, :],
                    owner,
                )

            return carry

        lax.fori_loop(0, n, each, 0)
        for offset in order:
            peer = partner(me, offset, n)

            @pl.when(far(peer))
            def _():
                out_copy(head, offset).start()

            @pl.when(extra(peer))
            def _():
                extra_copy(head, offset).start()

        @pl.when(far(me))
        def _():
            own_out(head).start()

        @pl.when(extra(me))
        def _():
            own_extra(head).start()

    @pl.when(me < n - 1)
    def _():
        above_copy.wait_recv()

    convolve_block(per_device)
    conv_out(row_count, BLOCK, 6).start()

    @pl.when(me < PAIR)
    def _():
        full_out.wait()

    for offset in [0] + order:

        @pl.when(far(me))
        def _():
            for head in range(head_count):
                if offset:
                    out_copy(head, offset).wait_recv()
                else:
                    own_out(head).wait()

        @pl.when(odd)
        def _():
            pass_copy(offset).start()

    @pl.when(extra(me))
    def _():
        for head in range(head_count):
            own_extra(head).wait()
            for offset in order:
                extra_copy(head, offset).wait_recv()

    for offset in [0] + order:

        @pl.when(odd)
        def _():
            pass_copy(offset).wait_send()

        @pl.when(jnp.logical_not(odd))
        def _():
            pass_copy(offset).wait_recv()

    for head in range(head_count):
        for offset in order:
            peer = partner(me, offset, n)

            @pl.when(far(peer))
            def _():
                out_copy(head, offset).wait_send()

            @pl.when(extra(peer))
            def _():
                extra_copy(head, offset).wait_send()

            for which in range(3):

                @pl.when(sends(which, me))
                def _():
                    qkv_copy(which, head, offset).wait_send()

    @pl.when(me == 0)
    def _():
        for copy in pair_copies:
            copy.wait_send()

    @pl.when(me < n - 1)
    def _():
        tail_copy.wait_send()

    @pl.when(me > 0)
    def _():
        above_copy.wait_send()

    conv_out(0, row_count, 5).wait()
    conv_out(row_count, BLOCK, 6).wait()


def exchange(n, queries, key_rows, values, inner_rows, conv_weight, conv_bias, info):
    row_count, features = queries.shape
    channels = inner_rows.shape[1]
    head_count = features // (n * D_HEAD)
    seq_len = n * row_count
    near = row_count + BLOCK
    chunk = PAIR * row_count
    dtype = queries.dtype
    hbm = pl.BlockSpec(memory_space=pl.ANY)
    vmem = pl.BlockSpec(memory_space=pltpu.VMEM)
    return pl.pallas_call(
        functools.partial(exchange_kernel, n, row_count, head_count),
        out_shape=(
            jax.ShapeDtypeStruct((near, features), dtype),
            jax.ShapeDtypeStruct((near, channels), dtype),
        ),
        in_specs=[hbm, hbm, hbm, hbm, vmem, vmem, vmem],
        out_specs=(hbm, hbm),
        scratch_shapes=[
            pltpu.VMEM((head_count, seq_len, D_HEAD), dtype),
            pltpu.VMEM((head_count, seq_len, D_HEAD), dtype),
            pltpu.VMEM((head_count, seq_len, D_HEAD), dtype),
            pltpu.VMEM((head_count, seq_len, D_HEAD), dtype),
            pltpu.VMEM((HALO + near, channels), dtype),
            pltpu.VMEM((near, channels), dtype),
            pltpu.VMEM((row_count, features), dtype),
            pltpu.VMEM((chunk, features), dtype),
            pltpu.VMEM((chunk, features), dtype),
            pltpu.VMEM((row_count, features), dtype),
            pltpu.VMEM((n,) + info.shape, jnp.int32),
            pltpu.VMEM((seq_len + BLOCK, LANES), jnp.int32),
            pltpu.VMEM((seq_len, LANES), jnp.int32),
            pltpu.VMEM((seq_len // chunk, row_count, chunk), jnp.float32),
            pltpu.SemaphoreType.DMA((3, head_count, n)),
            pltpu.SemaphoreType.DMA((3, head_count, n)),
            pltpu.SemaphoreType.DMA((head_count, n)),
            pltpu.SemaphoreType.DMA((head_count, n)),
            pltpu.SemaphoreType.DMA((head_count, n)),
            pltpu.SemaphoreType.DMA((head_count, n)),
            pltpu.SemaphoreType.DMA((n,)),
            pltpu.SemaphoreType.DMA((n,)),
            pltpu.SemaphoreType.DMA((8,)),
            pltpu.SemaphoreType.DMA((n,)),
            pltpu.SemaphoreType.DMA((n,)),
            pltpu.SemaphoreType.DMA((7,)),
            pltpu.SemaphoreType.DMA((5, head_count)),
        ],
        compiler_params=pltpu.CompilerParams(
            collective_id=0, has_side_effects=True, vmem_limit_bytes=56 * 1024 * 1024
        ),
    )(queries, key_rows, values, inner_rows, conv_weight, conv_bias, info)


def owned_kernel(counts_ref, here_ref, attn_ref, conv_ref, attn_out, conv_out, *, steps):
    own = counts_ref[here_ref[0]] * steps
    live = pl.program_id(0) < own

    @pl.when(live)
    def _():
        attn_out[...] = attn_ref[...]
        conv_out[...] = conv_ref[...]

    @pl.when(jnp.logical_not(live))
    def _():
        attn_out[...] = jnp.zeros_like(attn_out)
        conv_out[...] = jnp.zeros_like(conv_out)


def owned(n, per_device, owner_counts, here, attn_near, conv_near):
    near = attn_near.shape[0]
    steps = 2
    rows = BLOCK // steps
    last = near // rows - 1

    def source(i, counts, here):
        first = 0
        for device in range(n):
            first = first + jnp.where(device < here[0], counts[device], 0)
        moved = first - here[0] * per_device
        return (jnp.minimum(i + moved * steps, last), 0)

    shapes = (attn_near, conv_near)
    return pl.pallas_call(
        functools.partial(owned_kernel, steps=steps),
        out_shape=tuple(jax.ShapeDtypeStruct(a.shape, a.dtype) for a in shapes),
        grid_spec=pltpu.PrefetchScalarGridSpec(
            num_scalar_prefetch=2,
            grid=(near // rows,),
            in_specs=[pl.BlockSpec((rows, a.shape[1]), source) for a in shapes],
            out_specs=tuple(
                pl.BlockSpec((rows, a.shape[1]), lambda i, counts, here: (i, 0)) for a in shapes
            ),
        ),
    )(owner_counts, here[None], attn_near, conv_near)


def by_heads(
    queries,
    key_rows,
    values,
    inner_rows,
    conv_weight,
    conv_bias,
    segment_ids,
    block_reach,
    owner_counts,
):
    n = lax.axis_size("ctx")
    here = lax.axis_index("ctx")
    row_count = queries.shape[0]
    per_device = row_count // BLOCK
    info = jnp.concatenate(
        [
            segment_ids.reshape(per_device, BLOCK),
            jnp.broadcast_to(block_reach[:, None], (per_device, BLOCK)),
            jnp.zeros((-2 * per_device % 8, BLOCK), jnp.int32),
        ],
        axis=0,
    )
    attn_near, conv_near = exchange(
        n, queries, key_rows, values, inner_rows, conv_weight, conv_bias[None, :], info
    )
    return owned(n, per_device, owner_counts, here, attn_near, conv_near)


def plan(*args):
    n = lax.axis_size("ctx")
    row_count, features = args[0].shape
    heads = features // D_HEAD
    power = n > 2 and n & (n - 1) == 0
    near_layout = row_count // BLOCK + (row_count // BLOCK) // 2 == row_count // BLOCK + 1
    if power and near_layout and heads % n == 0 and n * row_count <= WINDOW:
        return by_heads(*args)
    return shards(*args)


def solution(mesh):
    return jax.shard_map(
        plan,
        mesh=mesh,
        in_specs=(
            P(("dp", "ctx"), None),
            P(("dp", "ctx"), None),
            P(("dp", "ctx"), None),
            P(("dp", "ctx"), None),
            P(),
            P(),
            P(("dp", "ctx")),
            P(("dp", "ctx")),
            P("dp"),
        ),
        out_specs=(P(("dp", "ctx"), None), P(("dp", "ctx"), None)),
        check_vma=False,
    )
```

```python
import functools
import math

import jax
import jax.numpy as jnp
from jax import lax
from jax.experimental import pallas as pl
from jax.experimental.pallas import tpu as pltpu
from jax.sharding import PartitionSpec as P

HEADS = 16
D_HEAD = 128
WINDOW = 2048
BLOCK = 128
KERNEL = 4


masked_score = -1e30


def from_behind(block, axis, distance):
    devices = range(lax.axis_size(axis))
    route = [(i - distance, i) for i in devices if i - distance in devices]
    return lax.ppermute(block, axis, route)


def attend(query_rows, key_span, value_span, query_seg, key_seg, block_first, reach_value):
    query_pos = block_first + jnp.arange(BLOCK, dtype=jnp.int32)
    key_pos = block_first - WINDOW + jnp.arange(WINDOW + BLOCK, dtype=jnp.int32)
    allowed = (key_pos[None, :] <= query_pos[:, None]) & (
        key_pos[None, :] > query_pos[:, None] - WINDOW
    )
    allowed = allowed & (key_pos[None, :] >= block_first - reach_value) & (key_pos[None, :] >= 0)
    allowed = allowed & (key_seg[None, :] == query_seg[:, None])
    heads_q = query_rows.reshape(BLOCK, HEADS, D_HEAD)
    heads_k = key_span.reshape(WINDOW + BLOCK, HEADS, D_HEAD)
    heads_v = value_span.reshape(WINDOW + BLOCK, HEADS, D_HEAD)
    scores = jnp.einsum("qhd,khd->hqk", heads_q, heads_k, preferred_element_type=jnp.float32) * (
        1.0 / math.sqrt(D_HEAD)
    )
    scores = jnp.where(allowed[None], scores, masked_score)
    row_top = jnp.max(scores, axis=2, keepdims=True)
    lifted = jnp.where(allowed[None], jnp.exp(scores - row_top), 0.0)
    weights = (lifted / jnp.sum(lifted, axis=2, keepdims=True)).astype(jnp.bfloat16)
    mixed = jnp.einsum("hqk,khd->qhd", weights, heads_v, preferred_element_type=jnp.float32)
    return mixed.reshape(BLOCK, HEADS * D_HEAD).astype(jnp.bfloat16)


def convolve(ext_rows, ext_seg, ext_pos, conv_weight, conv_bias, row_count):
    lag = KERNEL - 1
    running = jnp.zeros((row_count, conv_bias.shape[0]), jnp.float32) + conv_bias[None, :]
    for offset in range(KERNEL):
        shifted = ext_rows[lag - offset : lag - offset + row_count].astype(jnp.float32)
        usable = (ext_seg[lag - offset : lag - offset + row_count] == ext_seg[lag:]) & (
            ext_pos[lag - offset : lag - offset + row_count] >= 0
        )
        running = running + conv_weight[offset][None, :] * jnp.where(usable[:, None], shifted, 0.0)
    return jax.nn.silu(running).astype(jnp.bfloat16)


def shards(
    queries,
    key_rows,
    values,
    inner_rows,
    conv_weight,
    conv_bias,
    segment_ids,
    block_reach,
    owner_counts,
):
    here_index = lax.axis_index("ctx")
    row_count = queries.shape[0]
    features = queries.shape[1]
    channels = inner_rows.shape[1]
    per_device = row_count // BLOCK
    most_blocks = per_device + per_device // 2
    back = WINDOW // row_count
    lag = KERNEL - 1
    starts = jnp.cumsum(owner_counts) - owner_counts
    first_block = starts[here_index]
    own_blocks = owner_counts[here_index]
    live = jnp.arange(most_blocks * BLOCK, dtype=jnp.int32) < own_blocks * BLOCK
    far_keys = []
    far_values = []
    far_segments = []
    for distance in range(back, 0, -1):
        received = from_behind((key_rows, values, segment_ids), "ctx", distance)
        far_keys.append(received[0])
        far_values.append(received[1])
        far_segments.append(received[2])
    key_buffer = jnp.concatenate(far_keys + [key_rows], axis=0)
    value_buffer = jnp.concatenate(far_values + [values], axis=0)
    segment_buffer = jnp.concatenate(far_segments + [segment_ids], axis=0)
    key_anchor = (here_index - back) * row_count
    tail_rows, tail_segments = from_behind(
        (inner_rows[row_count - lag :], segment_ids[row_count - lag :]), "ctx", 1
    )

    def own_block(slot_index):
        local_first = slot_index * BLOCK
        block_first = here_index * row_count + local_first
        key_at = block_first - WINDOW - key_anchor
        return attend(
            lax.dynamic_slice_in_dim(queries, local_first, BLOCK, 0),
            lax.dynamic_slice_in_dim(key_buffer, key_at, WINDOW + BLOCK, 0),
            lax.dynamic_slice_in_dim(value_buffer, key_at, WINDOW + BLOCK, 0),
            lax.dynamic_slice_in_dim(segment_ids, local_first, BLOCK, 0),
            lax.dynamic_slice_in_dim(segment_buffer, key_at, WINDOW + BLOCK, 0),
            block_first,
            block_reach[slot_index],
        )

    attention_local = lax.map(own_block, jnp.arange(per_device, dtype=jnp.int32)).reshape(
        row_count, features
    )
    conv_local = convolve(
        jnp.concatenate([tail_rows, inner_rows], axis=0),
        jnp.concatenate([tail_segments, segment_ids], axis=0),
        here_index * row_count - lag + jnp.arange(row_count + lag, dtype=jnp.int32),
        conv_weight,
        conv_bias,
        row_count,
    )
    above = from_behind((attention_local, conv_local), "ctx", -1)
    attention_near = jnp.concatenate(
        [attention_local, above[0], jnp.zeros((row_count, features), jnp.bfloat16)], axis=0
    )
    conv_near = jnp.concatenate(
        [conv_local, above[1], jnp.zeros((row_count, channels), jnp.bfloat16)], axis=0
    )
    offset_rows = first_block * BLOCK - here_index * row_count
    attention_owned = lax.dynamic_slice_in_dim(attention_near, offset_rows, most_blocks * BLOCK, 0)
    conv_owned_rows = lax.dynamic_slice_in_dim(conv_near, offset_rows, most_blocks * BLOCK, 0)
    attention_owned = jnp.where(live[:, None], attention_owned, 0)
    conv_owned_rows = jnp.where(live[:, None], conv_owned_rows, 0)
    return (attention_owned, conv_owned_rows)


LANES = 128
HALO = 16
PAIR = 2
MESH = pl.DeviceIdType.MESH


def partner(me, offset, n):
    result, bit = 0, 1
    while bit < n:
        result = result + ((me // bit + offset // bit) % 2) * bit
        bit *= 2
    return result


def exchange_kernel(
    n,
    row_count,
    head_count,
    q_hbm,
    k_hbm,
    v_hbm,
    x_hbm,
    weight_ref,
    bias_ref,
    segment_ref,
    reach_ref,
    attn_near,
    conv_near,
    qr,
    kr,
    vr,
    ob,
    xb,
    conv_buf,
    q_full,
    k_full,
    v_full,
    o_full,
    info_ref,
    infos,
    start_ref,
    lo_ref,
    s_ref,
    qkv_send,
    qkv_recv,
    o_send,
    o_recv,
    extra_send,
    extra_recv,
    pass_send,
    pass_recv,
    full_sem,
    info_send,
    info_recv,
    halo_sem,
    local_sem,
):
    me = lax.axis_index("ctx")
    per_device = row_count // BLOCK
    seq_len = n * row_count
    channels = bias_ref.shape[1]
    chunk = s_ref.shape[2]
    scale = math.log2(math.e) / math.sqrt(D_HEAD)
    order = list(range(2, n)) + [1]

    info_ref[...] = jnp.zeros_like(info_ref)
    info_ref[pl.ds(0, per_device), :] = segment_ref[...]
    for part in range(per_device):
        info_ref[per_device + part : per_device + part + 1, :] = jnp.full(
            (1, LANES), reach_ref[part], jnp.int32
        )

    barrier = pltpu.get_barrier_semaphore()
    for offset in range(1, n):
        pl.semaphore_signal(
            barrier, inc=1, device_id={"ctx": partner(me, offset, n)}, device_id_type=MESH
        )
    pl.semaphore_wait(barrier, n - 1)

    def rows_of(device, count=row_count):
        return pl.ds(pl.multiple_of(device * row_count, BLOCK), count)

    def head_of(device, head):
        at = device * (head_count * D_HEAD) + head * D_HEAD
        return pl.ds(pl.multiple_of(at, D_HEAD), D_HEAD)

    def remote(src, dst, send, recv, device):
        return pltpu.make_async_remote_copy(
            src_ref=src,
            dst_ref=dst,
            send_sem=send,
            recv_sem=recv,
            device_id={"ctx": device},
            device_id_type=MESH,
        )

    def info_copy(offset):
        return remote(
            info_ref,
            infos.at[me],
            info_send.at[offset],
            info_recv.at[offset],
            partner(me, offset, n),
        )

    pairs = ((k_hbm, kr), (q_hbm, qr), (v_hbm, vr))

    def qkv_copy(which, head, offset):
        peer = partner(me, offset, n)
        src, dst = pairs[which]
        return remote(
            src.at[:, head_of(peer, head)],
            dst.at[head, rows_of(me)],
            qkv_send.at[which, head, offset],
            qkv_recv.at[which, head, offset],
            peer,
        )

    def own_copy(which, head):
        src, dst = pairs[which]
        return pltpu.make_async_copy(
            src.at[:, head_of(me, head)], dst.at[head, rows_of(me)], local_sem.at[which, head]
        )

    tail_copy = remote(
        x_hbm.at[pl.ds(row_count - HALO, HALO)],
        xb.at[pl.ds(0, HALO)],
        halo_sem.at[0],
        halo_sem.at[1],
        (me + 1) % n,
    )
    above_copy = remote(
        x_hbm.at[pl.ds(0, BLOCK)],
        xb.at[pl.ds(HALO + row_count, BLOCK)],
        halo_sem.at[2],
        halo_sem.at[3],
        (me + n - 1) % n,
    )
    full_copies = [
        pltpu.make_async_copy(q_hbm, q_full, full_sem.at[0]),
        pltpu.make_async_copy(k_hbm, k_full.at[rows_of(me % PAIR)], full_sem.at[1]),
        pltpu.make_async_copy(v_hbm, v_full.at[rows_of(me % PAIR)], full_sem.at[2]),
    ]
    pair_copies = [
        remote(
            src,
            dst.at[pl.ds(0, row_count)],
            full_sem.at[3 + 2 * i],
            full_sem.at[4 + 2 * i],
            partner(me, 1, n),
        )
        for i, (src, dst) in enumerate(((k_hbm, k_full), (v_hbm, v_full)))
    ]

    def sends(which, device):
        return device >= (PAIR if which == 1 else 0)

    own_rows = pltpu.make_async_copy(x_hbm, xb.at[pl.ds(HALO, row_count)], halo_sem.at[4])

    for offset in order:
        info_copy(offset).start()

    @pl.when(me < n - 1)
    def _():
        tail_copy.start()

    own_rows.start()
    @pl.when(me < PAIR)
    def _():
        for copy in full_copies:
            copy.start()

    @pl.when(me == 0)
    def _():
        for copy in pair_copies:
            copy.start()

    for head in range(head_count):
        for which in range(3):
            for offset in order:

                @pl.when(sends(which, me))
                def _():
                    qkv_copy(which, head, offset).start()

            own_copy(which, head).start()

    @pl.when(me > 0)
    def _():
        above_copy.start()

    infos[me] = info_ref[...]
    start_ref[pl.ds(seq_len, BLOCK), :] = jnp.zeros((BLOCK, LANES), jnp.int32)

    @pl.when(me == 0)
    def _():
        xb[pl.ds(0, HALO), :] = jnp.zeros((HALO, channels), xb.dtype)
        v_full[pl.ds(row_count, row_count), :] = jnp.zeros(q_full.shape, v_full.dtype)

    @pl.when(me == n - 1)
    def _():
        xb[pl.ds(HALO + row_count, BLOCK), :] = jnp.zeros((BLOCK, channels), xb.dtype)

    for offset in order:
        info_copy(offset).wait()

    def bounds(device, carry):
        for part in range(per_device):
            segs = jnp.broadcast_to(infos[device, part : part + 1, :], (BLOCK, LANES)).T
            reach = infos[device, per_device + part : per_device + part + 1, :]
            count = jnp.zeros((BLOCK, LANES), jnp.float32)
            for other in range(n):
                for row in range(per_device):
                    count = count + jnp.where(infos[other, row : row + 1, :] < segs, 1.0, 0.0)
            begin = jnp.broadcast_to(
                jnp.sum(count, axis=1, keepdims=True), (BLOCK, LANES)
            ).astype(jnp.int32)
            first = device * row_count + part * BLOCK
            at = pl.ds(pl.multiple_of(first, BLOCK), BLOCK)
            start_ref[at, :] = begin
            lo_ref[at, :] = jnp.maximum(begin, first - reach)
        return carry

    lax.fori_loop(0, n, bounds, 0)

    def convolve_block(block):
        first = me * row_count + block * BLOCK
        begin = start_ref[pl.ds(pl.multiple_of(first, BLOCK), BLOCK), :]
        place = first + lax.broadcasted_iota(jnp.int32, (BLOCK, LANES), 0) - begin

        def part(step, carry):
            cols = pl.ds(pl.multiple_of(step * LANES, LANES), LANES)
            rows = xb[pl.ds(block * BLOCK, BLOCK + HALO), cols].astype(jnp.float32)
            running = jnp.broadcast_to(bias_ref[:, cols], (BLOCK, LANES))
            for tap in range(KERNEL):
                moved = rows if tap == 0 else pltpu.roll(rows, tap, 0)
                moved = moved[HALO:]
                if tap:
                    moved = jnp.where(place >= tap, moved, 0.0)
                running = running + weight_ref[tap : tap + 1, cols] * moved
            gated = running / (1.0 + jnp.exp(-running))
            conv_buf[pl.ds(block * BLOCK, BLOCK), cols] = gated.astype(conv_buf.dtype)
            return carry

        lax.fori_loop(0, channels // LANES, part, 0)

    own_rows.wait()

    @pl.when(me > 0)
    def _():
        tail_copy.wait_recv()

    for block in range(per_device):
        convolve_block(block)

    def conv_out(at, count, sem):
        rows = pl.ds(at, count)
        return pltpu.make_async_copy(conv_buf.at[rows], conv_near.at[rows], halo_sem.at[sem])

    conv_out(0, row_count, 5).start()

    def attend_rows(q, keys_at, values_at, owner):
        lo = lo_ref[rows_of(owner), :]
        place = owner * row_count + lax.broadcasted_iota(jnp.int32, (row_count, LANES), 0)
        lane = lax.broadcasted_iota(jnp.int32, (row_count, LANES), 1)
        steps = (owner * row_count + row_count + chunk - 1) // chunk

        def score(step, top):
            keys = keys_at(pl.ds(pl.multiple_of(step * chunk, chunk), chunk))
            scores = lax.dot_general(
                q, keys, (((1,), (1,)), ((), ())), preferred_element_type=jnp.float32
            )
            for group in range(chunk // LANES):
                at = step * chunk + group * LANES + lane
                masked = jnp.where(
                    (at >= lo) & (at <= place),
                    scores[:, group * LANES : (group + 1) * LANES],
                    masked_score,
                )
                s_ref[step, :, pl.ds(group * LANES, LANES)] = masked
                top = jnp.maximum(top, masked)
            return top

        top = lax.fori_loop(
            0, steps, score, jnp.full((row_count, LANES), masked_score, jnp.float32)
        )
        top = jnp.broadcast_to(jnp.max(top, axis=1, keepdims=True), (row_count, LANES))

        def blend(step, carry):
            total, mixed = carry
            weights = []
            for group in range(chunk // LANES):
                scores = s_ref[step, :, pl.ds(group * LANES, LANES)]
                lifted = jnp.exp2((scores - top) * scale)
                total = total + lifted
                weights.append(lifted.astype(jnp.bfloat16))
            vals = values_at(pl.ds(pl.multiple_of(step * chunk, chunk), chunk))
            mixed = mixed + jnp.dot(
                jnp.concatenate(weights, axis=1), vals, preferred_element_type=jnp.float32
            )
            return total, mixed

        zero = jnp.zeros((row_count, LANES), jnp.float32)
        total, mixed = lax.fori_loop(0, steps, blend, (zero, zero))
        mixed = mixed / jnp.sum(total, axis=1, keepdims=True)
        return mixed.astype(jnp.bfloat16)

    own_rows_at = pl.ds(0, row_count)
    extra_at = pl.ds(row_count, BLOCK)
    full_out = pltpu.make_async_copy(o_full, attn_near.at[own_rows_at], full_sem.at[7])

    @pl.when(me < PAIR)
    def _():
        for copy in full_copies:
            copy.wait()

        @pl.when(me == 1)
        def _():
            for copy in pair_copies:
                copy.wait_recv()

        def each(head, carry):
            cols = pl.ds(pl.multiple_of(head * D_HEAD, D_HEAD), D_HEAD)
            o_full[:, cols] = attend_rows(
                q_full[:, cols], lambda at: k_full[at, cols], lambda at: v_full[at, cols], me
            )
            return carry

        lax.fori_loop(0, n * head_count, each, 0)
        full_out.start()

    def out_copy(head, offset):
        peer = partner(me, offset, n)
        return remote(
            ob.at[head, rows_of(peer)],
            attn_near.at[own_rows_at, head_of(me, head)],
            o_send.at[head, offset],
            o_recv.at[head, offset],
            peer,
        )

    def extra_copy(head, offset):
        peer = partner(me, offset, n)
        return remote(
            ob.at[head, rows_of((peer + 1) % n, BLOCK)],
            attn_near.at[extra_at, head_of(me, head)],
            extra_send.at[head, offset],
            extra_recv.at[head, offset],
            peer,
        )

    def own_out(head):
        return pltpu.make_async_copy(
            ob.at[head, rows_of(me)],
            attn_near.at[own_rows_at, head_of(me, head)],
            local_sem.at[3, head],
        )

    def own_extra(head):
        return pltpu.make_async_copy(
            ob.at[head, rows_of((me + 1) % n, BLOCK)],
            attn_near.at[extra_at, head_of(me, head)],
            local_sem.at[4, head],
        )

    def pass_copy(offset):
        at = partner(me, offset, n) * (head_count * D_HEAD)
        cols = pl.ds(pl.multiple_of(at, D_HEAD), head_count * D_HEAD)
        return remote(
            attn_near.at[pl.ds(0, BLOCK), cols],
            attn_near.at[extra_at, cols],
            pass_send.at[offset],
            pass_recv.at[offset],
            partner(me, 1, n),
        )

    def far(device):
        return device >= PAIR

    def extra(device):
        return (device % PAIR == PAIR - 1) & (device < n - 1)

    odd = me % PAIR == PAIR - 1

    for head in range(head_count):
        for which in range(3):
            own_copy(which, head).wait()
            for offset in order:

                @pl.when(sends(which, partner(me, offset, n)))
                def _():
                    qkv_copy(which, head, offset).wait_recv()

        def each(step, carry):
            owner = partner(me, (step + 2) % n, n)

            @pl.when(far(owner))
            def _():
                ob[head, rows_of(owner), :] = attend_rows(
                    qr[head, rows_of(owner), :],
                    lambda at: kr[head, at, :],
                    lambda at: vr[head, at, :],
                    owner,
                )

            return carry

        lax.fori_loop(0, n, each, 0)
        for offset in order:
            peer = partner(me, offset, n)

            @pl.when(far(peer))
            def _():
                out_copy(head, offset).start()

            @pl.when(extra(peer))
            def _():
                extra_copy(head, offset).start()

        @pl.when(far(me))
        def _():
            own_out(head).start()

        @pl.when(extra(me))
        def _():
            own_extra(head).start()

    @pl.when(me < n - 1)
    def _():
        above_copy.wait_recv()

    convolve_block(per_device)
    conv_out(row_count, BLOCK, 6).start()

    @pl.when(me < PAIR)
    def _():
        full_out.wait()

    for offset in [0] + order:

        @pl.when(far(me))
        def _():
            for head in range(head_count):
                if offset:
                    out_copy(head, offset).wait_recv()
                else:
                    own_out(head).wait()

        @pl.when(odd)
        def _():
            pass_copy(offset).start()

    @pl.when(extra(me))
    def _():
        for head in range(head_count):
            own_extra(head).wait()
            for offset in order:
                extra_copy(head, offset).wait_recv()

    for offset in [0] + order:

        @pl.when(odd)
        def _():
            pass_copy(offset).wait_send()

        @pl.when(jnp.logical_not(odd))
        def _():
            pass_copy(offset).wait_recv()

    for head in range(head_count):
        for offset in order:
            peer = partner(me, offset, n)

            @pl.when(far(peer))
            def _():
                out_copy(head, offset).wait_send()

            @pl.when(extra(peer))
            def _():
                extra_copy(head, offset).wait_send()

            for which in range(3):

                @pl.when(sends(which, me))
                def _():
                    qkv_copy(which, head, offset).wait_send()

    @pl.when(me == 0)
    def _():
        for copy in pair_copies:
            copy.wait_send()

    @pl.when(me < n - 1)
    def _():
        tail_copy.wait_send()

    @pl.when(me > 0)
    def _():
        above_copy.wait_send()

    conv_out(0, row_count, 5).wait()
    conv_out(row_count, BLOCK, 6).wait()


def exchange(
    n, queries, key_rows, values, inner_rows, conv_weight, conv_bias, segments, block_reach
):
    row_count, features = queries.shape
    channels = inner_rows.shape[1]
    head_count = features // (n * D_HEAD)
    seq_len = n * row_count
    near = row_count + BLOCK
    chunk = PAIR * row_count
    info_rows = pl.cdiv(2 * segments.shape[0], 8) * 8
    dtype = queries.dtype
    hbm = pl.BlockSpec(memory_space=pl.ANY)
    vmem = pl.BlockSpec(memory_space=pltpu.VMEM)
    return pl.pallas_call(
        functools.partial(exchange_kernel, n, row_count, head_count),
        out_shape=(
            jax.ShapeDtypeStruct((near, features), dtype),
            jax.ShapeDtypeStruct((near, channels), dtype),
        ),
        in_specs=[hbm, hbm, hbm, hbm, vmem, vmem, vmem, pl.BlockSpec(memory_space=pltpu.SMEM)],
        out_specs=(hbm, hbm),
        scratch_shapes=[
            pltpu.VMEM((head_count, seq_len, D_HEAD), dtype),
            pltpu.VMEM((head_count, seq_len, D_HEAD), dtype),
            pltpu.VMEM((head_count, seq_len, D_HEAD), dtype),
            pltpu.VMEM((head_count, seq_len, D_HEAD), dtype),
            pltpu.VMEM((HALO + near, channels), dtype),
            pltpu.VMEM((near, channels), dtype),
            pltpu.VMEM((row_count, features), dtype),
            pltpu.VMEM((chunk, features), dtype),
            pltpu.VMEM((chunk, features), dtype),
            pltpu.VMEM((row_count, features), dtype),
            pltpu.VMEM((info_rows, LANES), jnp.int32),
            pltpu.VMEM((n, info_rows, LANES), jnp.int32),
            pltpu.VMEM((seq_len + BLOCK, LANES), jnp.int32),
            pltpu.VMEM((seq_len, LANES), jnp.int32),
            pltpu.VMEM((seq_len // chunk, row_count, chunk), jnp.float32),
            pltpu.SemaphoreType.DMA((3, head_count, n)),
            pltpu.SemaphoreType.DMA((3, head_count, n)),
            pltpu.SemaphoreType.DMA((head_count, n)),
            pltpu.SemaphoreType.DMA((head_count, n)),
            pltpu.SemaphoreType.DMA((head_count, n)),
            pltpu.SemaphoreType.DMA((head_count, n)),
            pltpu.SemaphoreType.DMA((n,)),
            pltpu.SemaphoreType.DMA((n,)),
            pltpu.SemaphoreType.DMA((8,)),
            pltpu.SemaphoreType.DMA((n,)),
            pltpu.SemaphoreType.DMA((n,)),
            pltpu.SemaphoreType.DMA((7,)),
            pltpu.SemaphoreType.DMA((5, head_count)),
        ],
        compiler_params=pltpu.CompilerParams(
            collective_id=0, has_side_effects=True, vmem_limit_bytes=56 * 1024 * 1024
        ),
    )(queries, key_rows, values, inner_rows, conv_weight, conv_bias, segments, block_reach)


def owned_kernel(
    n, per_device, counts_ref, attn_near, conv_near, attn_out, conv_out, attn_buf, conv_buf, zero, sems
):
    here = lax.axis_index("ctx")
    first = 0
    for device in range(n):
        first = first + jnp.where(device < here, counts_ref[device], 0)
    moved = jnp.clip(first - here * per_device, 0, 1)
    own = counts_ref[here]
    blocks = attn_near.shape[0] // BLOCK
    trios = ((attn_near, attn_buf, attn_out), (conv_near, conv_buf, conv_out))

    def fetch(block, which):
        src, buf, _ = trios[which]
        at = pl.multiple_of(jnp.minimum(block + moved, blocks - 1) * BLOCK, BLOCK)
        return pltpu.make_async_copy(
            src.at[pl.ds(at, BLOCK)], buf.at[block], sems.at[0, which, block]
        )

    def store(block, which, source):
        dst = trios[which][2]
        return pltpu.make_async_copy(
            source, dst.at[pl.ds(block * BLOCK, BLOCK)], sems.at[1, which, block]
        )

    for block in range(blocks):

        @pl.when(block < own)
        def _():
            for which in range(2):
                fetch(block, which).start()

    zero[...] = jnp.zeros_like(zero)
    for block in range(blocks):

        @pl.when(block < own)
        def _():
            for which in range(2):
                fetch(block, which).wait()
                store(block, which, trios[which][1].at[block]).start()

        @pl.when(block >= own)
        def _():
            for which in range(2):
                width = trios[which][0].shape[1]
                store(block, which, zero.at[:, pl.ds(0, width)]).start()

    for block in range(blocks):
        for which in range(2):
            store(block, which, trios[which][1].at[block]).wait()


def owned(n, per_device, owner_counts, attn_near, conv_near):
    near = attn_near.shape[0]
    blocks = near // BLOCK
    widths = [a.shape[1] for a in (attn_near, conv_near)]
    hbm = pl.BlockSpec(memory_space=pl.ANY)
    return pl.pallas_call(
        functools.partial(owned_kernel, n, per_device),
        out_shape=tuple(jax.ShapeDtypeStruct(a.shape, a.dtype) for a in (attn_near, conv_near)),
        in_specs=[pl.BlockSpec(memory_space=pltpu.SMEM), hbm, hbm],
        out_specs=(hbm, hbm),
        scratch_shapes=[
            pltpu.VMEM((blocks, BLOCK, widths[0]), attn_near.dtype),
            pltpu.VMEM((blocks, BLOCK, widths[1]), conv_near.dtype),
            pltpu.VMEM((BLOCK, max(widths)), attn_near.dtype),
            pltpu.SemaphoreType.DMA((2, 2, blocks)),
        ],
    )(owner_counts, attn_near, conv_near)


def by_heads(
    queries,
    key_rows,
    values,
    inner_rows,
    conv_weight,
    conv_bias,
    segment_ids,
    block_reach,
    owner_counts,
):
    n = lax.axis_size("ctx")
    row_count = queries.shape[0]
    per_device = row_count // BLOCK
    attn_near, conv_near = exchange(
        n,
        queries,
        key_rows,
        values,
        inner_rows,
        conv_weight,
        conv_bias[None, :],
        segment_ids.reshape(per_device, BLOCK),
        block_reach,
    )
    return owned(n, per_device, owner_counts, attn_near, conv_near)


def plan(*args):
    n = lax.axis_size("ctx")
    row_count, features = args[0].shape
    heads = features // D_HEAD
    power = n > 2 and n & (n - 1) == 0
    near_layout = row_count // BLOCK + (row_count // BLOCK) // 2 == row_count // BLOCK + 1
    if power and near_layout and heads % n == 0 and n * row_count <= WINDOW:
        return by_heads(*args)
    return shards(*args)


def solution(mesh):
    return jax.shard_map(
        plan,
        mesh=mesh,
        in_specs=(
            P(("dp", "ctx"), None),
            P(("dp", "ctx"), None),
            P(("dp", "ctx"), None),
            P(("dp", "ctx"), None),
            P(),
            P(),
            P(("dp", "ctx")),
            P(("dp", "ctx")),
            P("dp"),
        ),
        out_specs=(P(("dp", "ctx"), None), P(("dp", "ctx"), None)),
        check_vma=False,
    )
```
